32 devices in a mesh: tok: 2 (over y), hid: 16 (over z, x, core).
Axes of the slice: x: 2, y: 2, z: 4, core: 2. Of those that a mesh axis runs over, the one named last changes fastest.
Arguments:
- student_in: bfloat16 [256, 8192], P('hid', 'tok'), may hold values from -6 to 6
- target_delta: bfloat16 [256, 8192], P('hid', 'tok'), may hold values from -3 to 3
- gate_weight: bfloat16 [8192, 16384], P('tok', 'hid'), may hold values from -0.0625 to 0.0625
- up_weight: bfloat16 [8192, 16384], P('tok', 'hid'), may hold values from -0.0625 to 0.0625
- down_weight: bfloat16 [16384, 8192], P('hid', 'tok'), may hold values from -0.046875 to 0.046875
- block_mask: int32 [3, 64, 128], P(None, 'tok', 'hid'), may hold values from 0 to 1, as said below
Outputs:
- student_out: bfloat16 [256, 8192], P('hid', 'tok')
- input_grad: bfloat16 [256, 8192], P('hid', 'tok')
- gate_wgrad: float32 [8192, 16384], P('tok', 'hid')
- up_wgrad: float32 [8192, 16384], P('tok', 'hid')
- down_wgrad: float32 [16384, 8192], P('hid', 'tok')
The draws below stay inside these ranges and needn't reach their ends.
Inputs may be any that keep to these rules, and one draw needn't show every extreme that they name: `block_mask`: each entry is 0 or 1 (1 keeps a 128 x 128 block of weights); the share of ones differs from one block column of hidden units to another.
All inputs are finite; a program needn't handle non-finite values.
Results may differ from the reference program's by a relative error of at most 0.0056.
Values may be sent and summed in bfloat16 or wider, within the bound.
No kernel may reach another device: no remote copies, remote signals or barrier semaphores. Data moves between devices by JAX's collectives and lax.ppermute only.
A program may use at most 192 MiB of HBM per device.

```python
import jax
import jax.numpy as jnp
from jax import lax

D = 8192
FF = 16384
BLOCK = 128
TOKENS = 256


def draw_block_mask(key, part):
    level_key, coin_key = jax.random.split(jax.random.fold_in(key, 17))
    levels = jax.random.randint(level_key, (3, 1, FF // BLOCK), 1, 8)
    coins = jax.random.randint(coin_key, (3, D // BLOCK, FF // BLOCK), 0, 8)
    return (coins < levels).astype(jnp.int32)


def level_of(rng, dims, cuts, least, top_value):
    gain = 1.0
    for position, parts in cuts:
        draws = jax.random.uniform(jax.random.fold_in(jax.random.fold_in(rng, 6), position), (parts,), jnp.float32, least / len(cuts), top_value / len(cuts))
        gain = gain * jnp.repeat(jnp.exp(draws), dims[position] // parts).reshape((-1,) + (1,) * (len(dims) - 1 - position))
    return gain


def bell_draw(stream_key, shape, spread, bound, cuts=(), dtype=jnp.bfloat16):
    values = jax.random.normal(stream_key, shape, jnp.float32) * spread
    if len(cuts) > 0:
        values = level_of(stream_key, shape, cuts, -0.22, 0.18) * values
    return jnp.clip(values, min=-bound, max=bound).astype(dtype)


def setup_inputs(seed: int = 0) -> dict:
    key_of = jax.random.split(jax.random.key(seed), 7)
    return {
        "student_in": bell_draw(key_of[0], (TOKENS, D), 1.0, 6.0, ((0, 16), (1, 2))),
        "target_delta": bell_draw(key_of[1], (TOKENS, D), 0.5, 3.0, ((0, 16), (1, 2))),
        "gate_weight": bell_draw(key_of[2], (D, FF), D ** -0.5, 0.0625, ((0, 2), (1, 16))),
        "up_weight": bell_draw(key_of[3], (D, FF), D ** -0.5, 0.0625, ((0, 2), (1, 16))),
        "down_weight": bell_draw(key_of[4], (FF, D), FF ** -0.5, 0.046875, ((0, 16), (1, 2))),
        "block_mask": draw_block_mask(jax.random.fold_in(key_of[6], 71), 0),
    }


def widen(blocks):
    return jnp.repeat(jnp.repeat(blocks, BLOCK, axis=0), BLOCK, axis=1)

def reference(student_in, target_delta, gate_weight, up_weight, down_weight, block_mask):
    gate_mask = widen(block_mask[0]).astype(jnp.bfloat16)
    up_mask = widen(block_mask[1]).astype(jnp.bfloat16)
    down_mask = widen(block_mask[2]).T.astype(jnp.bfloat16)
    gate_eff = gate_weight * gate_mask
    up_eff = up_weight * up_mask
    down_eff = down_weight * down_mask
    gate = jnp.dot(student_in, gate_eff, preferred_element_type=jnp.float32)
    up = jnp.dot(student_in, up_eff, preferred_element_type=jnp.float32)
    sigma = jax.nn.sigmoid(gate)
    swish = gate * sigma
    hidden = (swish * up).astype(jnp.bfloat16)
    output_sum = jnp.dot(hidden, down_eff, preferred_element_type=jnp.float32)
    error = (output_sum - target_delta.astype(jnp.float32)).astype(jnp.bfloat16)
    by_cols = (((1,), (1,)), ((), ()))
    by_rows = (((0,), (0,)), ((), ()))
    hidden_grad = lax.dot_general(error, down_eff, by_cols, preferred_element_type=jnp.float32)
    gate_grad = (hidden_grad * up * (sigma + gate * sigma * (1.0 - sigma))).astype(jnp.bfloat16)
    up_grad = (hidden_grad * swish).astype(jnp.bfloat16)
    factor = 1.0 / jnp.sqrt(jnp.float32(TOKENS))
    gate_wgrad = lax.dot_general(student_in, gate_grad, by_rows, preferred_element_type=jnp.float32) * gate_mask.astype(jnp.float32) * factor
    up_wgrad = lax.dot_general(student_in, up_grad, by_rows, preferred_element_type=jnp.float32) * up_mask.astype(jnp.float32) * factor
    down_wgrad = lax.dot_general(hidden, error, by_rows, preferred_element_type=jnp.float32) * down_mask.astype(jnp.float32) * factor
    input_grad = lax.dot_general(gate_grad, gate_eff, by_cols, preferred_element_type=jnp.float32)
    input_grad = input_grad + lax.dot_general(up_grad, up_eff, by_cols, preferred_element_type=jnp.float32)
    return (output_sum.astype(jnp.bfloat16), input_grad.astype(jnp.bfloat16), gate_wgrad, up_wgrad, down_wgrad)
```

```python
import functools

import jax
import jax.numpy as jnp
from jax import lax
from jax.experimental import pallas as pl
from jax.experimental.pallas import tpu as pltpu
from jax.sharding import PartitionSpec as P


BLOCK = 128
CORES = 2
F32, BF16 = jnp.float32, jnp.bfloat16
BY_COLS = (((1,), (1,)), ((), ()))
BY_ROWS = (((0,), (0,)), ((), ()))
VMEM_LIMIT = 48 * 2**20


def swap(x, axis, offset):
    n = lax.axis_size(axis)
    return lax.ppermute(x, axis, [(i, i ^ offset) for i in range(n)])


def shifts(x):
    n = lax.axis_size("tok")
    return [lax.ppermute(x, "tok", [(i, (i + d) % n) for i in range(n)]) for d in range(1, n)]


def masked(w_ref, m_ref):
    parts = [
        w_ref[j * BLOCK : (j + 1) * BLOCK, :] * jnp.broadcast_to(m_ref[j].astype(BF16), (BLOCK, w_ref.shape[1]))
        for j in range(w_ref.shape[0] // BLOCK)
    ]
    return jnp.concatenate(parts, axis=0)


def call(body, name, grid, in_specs, out_specs, out_shape, scratch, args, flops):
    moved = sum(a.size * a.dtype.itemsize for a in args)
    moved += sum(o.size * jnp.dtype(o.dtype).itemsize for o in out_shape)
    return pl.pallas_call(
        body,
        name=name,
        grid=grid,
        in_specs=in_specs,
        out_specs=out_specs,
        out_shape=out_shape,
        scratch_shapes=scratch,
        cost_estimate=pl.CostEstimate(flops=flops, bytes_accessed=moved, transcendentals=0),
        compiler_params=pltpu.CompilerParams(
            dimension_semantics=("arbitrary",) * len(grid), vmem_limit_bytes=VMEM_LIMIT
        ),
    )(*args)


def whole(a):
    return pl.BlockSpec(a.shape, lambda i: (0,) * a.ndim)


def sds(shape, dtype):
    return jax.ShapeDtypeStruct(shape, dtype)


def gate_up_body(x0, x1, gw, uw, gm, um, own, send):
    step = pl.program_id(0)
    x = jnp.concatenate([x0[...], x1[...]], axis=0)
    f = gw.shape[1]

    @pl.when(step == 0)
    def _():
        own[...] = jnp.zeros_like(own)

    own[:, :f] += jnp.dot(x, masked(gw, gm), preferred_element_type=F32)
    own[:, f:] += jnp.dot(x, masked(uw, um), preferred_element_type=F32)

    @pl.when(step == pl.num_programs(0) - 1)
    def _():
        send[...] = own[...].astype(BF16)


def gate_up(x0, x1, gw, uw, gm, um):
    d, f = gw.shape
    m, kb = 2 * x0.shape[0], min(512, d)
    xs = pl.BlockSpec((m // 2, kb), lambda i: (0, i))
    ws = pl.BlockSpec((kb, f), lambda i: (i, 0))
    ms = pl.BlockSpec((kb // BLOCK, 1, f), lambda i: (i, 0, 0))
    outs = [sds((m, 2 * f), F32), sds((m, 2 * f), BF16)]
    return call(
        gate_up_body, "gate_up", (d // kb,), [xs, xs, ws, ws, ms, ms], [whole(o) for o in outs], outs, [],
        (x0, x1, gw, uw, gm, um), 4 * m * d * f,
    )


def total(own, recvs):
    out = own[...]
    for r in recvs:
        out = out + r[...].astype(F32)
    return out


def down_body(n, *refs):
    og, ou = refs[:2]
    rg, ru = refs[2 : 2 + n], refs[2 + n : 2 + 2 * n]
    dw, dm, hidden, own, send, acc = refs[2 + 2 * n :]
    step = pl.program_id(0)
    gate, up = total(og, rg), total(ou, ru)
    sigma = jax.nn.sigmoid(gate)
    h = (gate * sigma * up).astype(BF16)
    hidden[...] = h
    part = jnp.dot(h, masked(dw, dm), preferred_element_type=F32)

    @pl.when(step == 0)
    def _():
        acc[...] = part

    @pl.when(step > 0)
    def _():
        acc[...] += part

    @pl.when(step == pl.num_programs(0) - 1)
    def _():
        half = own.shape[0]
        own[...] = acc[:half, :]
        send[...] = acc[half:, :].astype(BF16)


def down(own, recvs, dw, dm):
    f, d = dw.shape
    m, fb = own.shape[0], min(256, f)
    steps = f // fb
    gs = pl.BlockSpec((m, fb), lambda i: (0, i))
    us = pl.BlockSpec((m, fb), lambda i: (0, steps + i))
    ws = pl.BlockSpec((fb, d), lambda i: (i, 0))
    ms = pl.BlockSpec((fb // BLOCK, 1, d), lambda i: (i, 0, 0))
    n = len(recvs)
    outs = [sds((m, f), BF16), sds((m // 2, d), F32), sds((m // 2, d), BF16)]
    return call(
        functools.partial(down_body, n), "down", (steps,),
        [gs, us] + [gs] * n + [us] * n + [ws, ms], [gs, whole(outs[1]), whole(outs[2])], outs,
        [pltpu.VMEM((m, d), F32)], (own, own, *recvs, *recvs, dw, dm), 2 * m * d * f,
    )


def hidden_grad_body(e0, e1, dw, dm, own, send, e):
    @pl.when(pl.program_id(0) == 0)
    def _():
        half = e0.shape[0]
        e[:half, :] = e0[...]
        e[half:, :] = e1[...]

    part = lax.dot_general(e[...], masked(dw, dm), BY_COLS, preferred_element_type=F32)
    own[...] = part
    send[...] = part.astype(BF16)


def hidden_grad(e0, e1, dw, dm):
    f, d = dw.shape
    m, fb = 2 * e0.shape[0], min(256, f)
    ws = pl.BlockSpec((fb, d), lambda i: (i, 0))
    ms = pl.BlockSpec((fb // BLOCK, 1, d), lambda i: (i, 0, 0))
    os = pl.BlockSpec((m, fb), lambda i: (0, i))
    return call(
        hidden_grad_body, "hidden_grad", (f // fb,), [whole(e0), whole(e1), ws, ms], [os, os],
        [sds((m, f), F32), sds((m, f), BF16)], [pltpu.VMEM((m, d), BF16)], (e0, e1, dw, dm), 2 * m * d * f,
    )


def input_grad_body(n, *refs):
    act, hid = refs[0], refs[1]
    ract, rhid = refs[2 : 2 + n], refs[2 + n : 2 + 2 * n]
    gw, uw, gm, um, gg, ug, own, send = refs[2 + 2 * n :]
    f = gw.shape[1]

    @pl.when(pl.program_id(0) == 0)
    def _():
        both, hg = total(act, ract), total(hid, rhid)
        gate, up = both[:, :f], both[:, f:]
        sigma = jax.nn.sigmoid(gate)
        swish = gate * sigma
        gg[...] = (hg * up * (sigma + swish * (1.0 - sigma))).astype(BF16)
        ug[...] = (hg * swish).astype(BF16)

    part = lax.dot_general(gg[...], masked(gw, gm), BY_COLS, preferred_element_type=F32)
    part += lax.dot_general(ug[...], masked(uw, um), BY_COLS, preferred_element_type=F32)
    half = own.shape[0]
    own[...] = part[:half, :]
    send[...] = part[half:, :].astype(BF16)


def input_grad(act, ract, hid, rhid, gw, uw, gm, um):
    d, f = gw.shape
    m, kb = act.shape[0], min(512, d)
    n = len(ract)
    ws = pl.BlockSpec((kb, f), lambda i: (i, 0))
    ms = pl.BlockSpec((kb // BLOCK, 1, f), lambda i: (i, 0, 0))
    os = pl.BlockSpec((m // 2, kb), lambda i: (0, i))
    outs = [sds((m, f), BF16), sds((m, f), BF16), sds((m // 2, d), F32), sds((m // 2, d), BF16)]
    args = (act, hid, *ract, *rhid, gw, uw, gm, um)
    return call(
        functools.partial(input_grad_body, n), "input_grad", (d // kb,),
        [whole(a) for a in args[: 2 + 2 * n]] + [ws, ws, ms, ms], [whole(outs[0]), whole(outs[1]), os, os],
        outs, [], args, 4 * m * d * f,
    )


def stack(dst, pieces):
    row = 0
    for p in pieces:
        dst[row : row + p.shape[0], :] = p[...]
        row += p.shape[0]


def down_wgrad_body(n, factor, *refs):
    hs, es = refs[:n], refs[n : 3 * n]
    dm, out, e = refs[3 * n :]

    @pl.when(pl.program_id(0) == 0)
    def _():
        stack(e, es)

    h = jnp.concatenate([r[...] for r in hs], axis=0)
    w = lax.dot_general(h, e[...], BY_ROWS, preferred_element_type=F32)
    for j in range(out.shape[0] // BLOCK):
        rows = slice(j * BLOCK, (j + 1) * BLOCK)
        out[rows, :] = w[rows, :] * (dm[j] * factor)


def down_wgrad(hs, es, dm, factor):
    m, f = hs[0].shape
    d, n = es[0].shape[1], len(hs)
    fb = BLOCK
    hspec = pl.BlockSpec((m, fb), lambda i: (0, i))
    return call(
        functools.partial(down_wgrad_body, n, factor), "down_wgrad", (f // fb,),
        [hspec] * n + [whole(e) for e in es] + [pl.BlockSpec((fb // BLOCK, 1, d), lambda i: (i, 0, 0))],
        [pl.BlockSpec((fb, d), lambda i: (i, 0))], [sds((f, d), F32)], [pltpu.VMEM((n * m, d), BF16)],
        (*hs, *es, dm), 2 * n * m * d * f,
    )[0]


def in_wgrad_body(n, factor, *refs):
    xs, ggs, ugs = refs[: 2 * n], refs[2 * n : 3 * n], refs[3 * n : 4 * n]
    gm, um, gout, uout, gg, ug = refs[4 * n :]

    @pl.when(pl.program_id(0) == 0)
    def _():
        stack(gg, ggs)
        stack(ug, ugs)

    x = jnp.concatenate([r[...] for r in xs], axis=0)
    for g, mask, out in ((gg, gm, gout), (ug, um, uout)):
        w = lax.dot_general(x, g[...], BY_ROWS, preferred_element_type=F32)
        for j in range(out.shape[0] // BLOCK):
            rows = slice(j * BLOCK, (j + 1) * BLOCK)
            out[rows, :] = w[rows, :] * (mask[j] * factor)


def in_wgrad(xs, ggs, ugs, gm, um, factor):
    n, (m, f) = len(ggs), ggs[0].shape
    d = xs[0].shape[1]
    kb = min(256, d)
    xspec = pl.BlockSpec((m // 2, kb), lambda i: (0, i))
    mspec = pl.BlockSpec((kb // BLOCK, 1, f), lambda i: (i, 0, 0))
    ospec = pl.BlockSpec((kb, f), lambda i: (i, 0))
    return call(
        functools.partial(in_wgrad_body, n, factor), "in_wgrad", (d // kb,),
        [xspec] * (2 * n) + [whole(g) for g in (*ggs, *ugs)] + [mspec, mspec], [ospec, ospec],
        [sds((d, f), F32)] * 2, [pltpu.VMEM((n * m, f), BF16)] * 2,
        (*xs, *ggs, *ugs, gm, um), 4 * n * m * d * f,
    )


def gather(shard, zs, xs):
    column = [shard] + [swap(shard, "hid", z) for z in zs]
    groups = [column] + [[swap(p, "hid", x) for p in column] for x in xs]
    halves = [jnp.concatenate(g, axis=0) for g in groups]
    return [(h, swap(h, "hid", 1)) for h in halves]


def scatter_group(own, recv, zs):
    rows = own.shape[0] // (len(zs) + 1)
    part = own + recv.astype(F32)
    out = part[:rows]
    for k, z in enumerate(zs):
        piece = part[(k + 1) * rows : (k + 2) * rows].astype(BF16)
        out = out + swap(piece, "hid", z).astype(F32)
    return out


def scatter(parts, zs, xs):
    cols = [scatter_group(own, swap(send, "hid", 1), zs) for own, send in parts]
    out = cols[0]
    for col, x in zip(cols[1:], xs):
        out = out + swap(col.astype(BF16), "hid", x).astype(F32)
    return out


def per_device(student_in, target_delta, gw, uw, dw, block_mask):
    hid = lax.axis_size("hid")
    nz = 4 if hid % 8 == 0 else 1
    nx = hid // (nz * CORES)
    zs = [k * nx * CORES for k in range(1, nz)]
    xs = [j * CORES for j in range(1, nx)]
    factor = float((student_in.shape[0] * hid) ** -0.5)

    def wide(b):
        return jnp.repeat(b.astype(F32), BLOCK, axis=1)[:, None, :]

    gm, um, dm = wide(block_mask[0]), wide(block_mask[1]), wide(block_mask[2].T)

    inputs = gather(student_in, zs, xs)
    acts = []
    for x0, x1 in inputs:
        own, send = gate_up(x0, x1, gw, uw, gm, um)
        acts.append((own, shifts(send)))
    hiddens, parts = [], []
    for own, recvs in acts:
        h, o, s = down(own, recvs, dw, dm)
        hiddens.append(h)
        parts.append((o, s))
    output_sum = scatter(parts, zs, xs)
    error = (output_sum - target_delta.astype(F32)).astype(BF16)
    errors = gather(error, zs, xs)
    hgs = []
    for e0, e1 in errors:
        own, send = hidden_grad(e0, e1, dw, dm)
        hgs.append((own, shifts(send)))
    ggs, ugs, parts = [], [], []
    for (act, ract), (hg, rhg) in zip(acts, hgs):
        gg, ug, o, s = input_grad(act, ract, hg, rhg, gw, uw, gm, um)
        ggs.append(gg)
        ugs.append(ug)
        parts.append((o, s))
    down_w = down_wgrad(hiddens, [p for e in errors for p in e], dm, factor)
    gate_w, up_w = in_wgrad([p for x in inputs for p in x], ggs, ugs, gm, um, factor)
    grad = scatter(parts, zs, xs)
    return (output_sum.astype(BF16), grad.astype(BF16), gate_w, up_w, down_w)


def solution(mesh):
    placed = (
        P("hid", "tok"),
        P("hid", "tok"),
        P("tok", "hid"),
        P("tok", "hid"),
        P("hid", "tok"),
        P(None, "tok", "hid"),
    )
    return jax.shard_map(
        per_device,
        mesh=mesh,
        in_specs=placed,
        out_specs=(
            P("hid", "tok"),
            P("hid", "tok"),
            P("tok", "hid"),
            P("tok", "hid"),
            P("hid", "tok"),
        ),
        check_vma=False,
    )
```

```python
import functools
import math

import jax
import jax.numpy as jnp
from jax import lax
from jax.experimental import pallas as pl
from jax.experimental.pallas import tpu as pltpu
from jax.sharding import PartitionSpec as P


BLOCK = 128
CORES = 2
F32, BF16 = jnp.float32, jnp.bfloat16
BY_COLS = (((1,), (1,)), ((), ()))
BY_ROWS = (((0,), (0,)), ((), ()))
MIB = 2**20
VM = pl.BlockSpec(memory_space=pltpu.VMEM)
HB = pl.BlockSpec(memory_space=pl.ANY)


def swap(x, axis, offset):
    n = lax.axis_size(axis)
    return lax.ppermute(x, axis, [(i, i ^ offset) for i in range(n)])


def shifts(x):
    n = lax.axis_size("tok")
    return [lax.ppermute(x, "tok", [(i, (i + d) % n) for i in range(n)]) for d in range(1, n)]


def sds(shape, dtype):
    return jax.ShapeDtypeStruct(shape, dtype)


def call(body, outs, args, flops, in_specs=None, out_specs=None, grid=(), scratch=(), limit=8, effects=False, aliases=None):
    moved = sum(a.size * a.dtype.itemsize for a in args)
    moved += sum(math.prod(o.shape) * jnp.dtype(o.dtype).itemsize for o in outs)
    return pl.pallas_call(
        body,
        grid=grid,
        in_specs=in_specs or [VM] * len(args),
        out_specs=out_specs or [VM] * len(outs),
        out_shape=outs,
        scratch_shapes=list(scratch),
        input_output_aliases=aliases or {},
        cost_estimate=pl.CostEstimate(flops=flops, bytes_accessed=moved, transcendentals=0),
        compiler_params=pltpu.CompilerParams(
            vmem_limit_bytes=limit * MIB,
            has_side_effects=effects,
            dimension_semantics=("arbitrary",) * len(grid) if grid else None,
        ),
    )(*args)


def vm(a):
    return pltpu.with_memory_space_constraint(a, pltpu.VMEM)


def whole(a):
    return pl.BlockSpec(a.shape, lambda i: (0,) * a.ndim)


def load_body(w, m, out, sems):
    n = sems.shape[0]
    rows = w.shape[0] // n
    copies = [
        pltpu.make_async_copy(w.at[pl.ds(j * rows, rows), :], out.at[pl.ds(j * rows, rows), :], sems.at[j])
        for j in range(n)
    ]
    for c in copies:
        c.start()
    for j in range(n):
        copies[j].wait()

        @pl.loop(0, rows // BLOCK)
        def _(i):
            k = j * (rows // BLOCK) + i
            at = pl.ds(pl.multiple_of(k * BLOCK, BLOCK), BLOCK)
            out[at, :] = out[at, :] * jnp.broadcast_to(m[k].astype(BF16), (BLOCK, w.shape[1]))


def load(w, m):
    parts = 4 if w.shape[0] % (4 * BLOCK) == 0 else 1
    return call(
        load_body, [pltpu.VMEM(w.shape, BF16)], (pltpu.with_memory_space_constraint(w, pltpu.HBM), m), 0,
        in_specs=[HB, VM], scratch=[pltpu.SemaphoreType.DMA((parts,))], limit=4,
    )[0]


def tick_body(x, out):
    out[...] = jnp.zeros_like(out)


def tick(x):
    return call(tick_body, [pltpu.VMEM((8, BLOCK), F32)], (x,), 0, in_specs=[HB], limit=1, effects=True)


def gate_up_body(x0, x1, ge, ue, own, send):
    x = jnp.concatenate([x0[...], x1[...]], axis=0)
    f = ge.shape[1]
    for w, off in ((ge, 0), (ue, f)):
        part = jnp.dot(x, w[...], preferred_element_type=F32)
        own[:, off : off + f] = part
        send[:, off : off + f] = part.astype(BF16)


def gate_up(x0, x1, ge, ue):
    d, f = ge.shape
    m = 2 * x0.shape[0]
    outs = [sds((m, 2 * f), F32), sds((m, 2 * f), BF16)]
    return call(gate_up_body, outs, (x0, x1, vm(ge), vm(ue)), 4 * m * d * f)


def total(own, recvs):
    out = own[...]
    for r in recvs:
        out = out + r[...].astype(F32)
    return out


def columns(d, n):
    return [slice(c, min(c + n, d)) for c in range(0, d, n)]


def down_body(n, *refs):
    act, recvs = refs[0], refs[1 : 1 + n]
    de, hidden, own, send = refs[1 + n :]
    f, d = de.shape
    both = total(act, recvs)
    gate, up = both[:, :f], both[:, f:]
    h = (gate * jax.nn.sigmoid(gate) * up).astype(BF16)
    hidden[...] = h
    half = own.shape[0]
    for c in columns(d, 1024):
        part = jnp.dot(h, de[:, c], preferred_element_type=F32)
        own[:, c] = part[:half]
        send[:, c] = part[half:].astype(BF16)


def down(act, recvs, de):
    f, d = de.shape
    m = act.shape[0]
    outs = [sds((m, f), BF16), sds((m // 2, d), F32), sds((m // 2, d), BF16)]
    return call(functools.partial(down_body, len(recvs)), outs, (act, *recvs, vm(de)), 2 * m * d * f)


def hidden_grad_body(e0, e1, de, own, send):
    e = jnp.concatenate([e0[...], e1[...]], axis=0)
    for c in columns(de.shape[0], 512):
        part = lax.dot_general(de[c, :], e, BY_COLS, preferred_element_type=F32).T
        own[:, c] = part
        send[:, c] = part.astype(BF16)


def hidden_grad(e0, e1, de):
    f, d = de.shape
    m = 2 * e0.shape[0]
    outs = [sds((m, f), F32), sds((m, f), BF16)]
    return call(hidden_grad_body, outs, (e0, e1, vm(de)), 2 * m * d * f)


def stack(dst, pieces):
    row = 0
    for p in pieces:
        dst[row : row + p.shape[0], :] = p[...]
        row += p.shape[0]


def wgrad_block(ls, right, c, mask, factor, store):
    left = jnp.concatenate([l[:, c] for l in ls], axis=0)
    w = lax.dot_general(left, right[...], BY_ROWS, preferred_element_type=F32)
    for k in range((c.stop - c.start) // BLOCK):
        rows = slice(k * BLOCK, (k + 1) * BLOCK)
        store(rows, w[rows, :] * (mask[c.start // BLOCK + k] * factor))


def input_grad_body(groups, n, *refs):
    acts, refs = [refs[g * (1 + n) : (g + 1) * (1 + n)] for g in range(groups)], refs[groups * (1 + n) :]
    hids, refs = [refs[g * (1 + n) : (g + 1) * (1 + n)] for g in range(groups)], refs[groups * (1 + n) :]
    ge, ue, gg_ref, ug_ref = refs[:4]
    owns, sends = refs[4 : 4 + groups], refs[4 + groups :]
    d, f = ge.shape
    m = gg_ref.shape[0] // groups
    for g, (act, hid) in enumerate(zip(acts, hids)):
        both, hg = total(act[0], act[1:]), total(hid[0], hid[1:])
        gate, up = both[:, :f], both[:, f:]
        sigma = jax.nn.sigmoid(gate)
        swish = gate * sigma
        gg_ref[g * m : (g + 1) * m, :] = (hg * up * (sigma + swish * (1.0 - sigma))).astype(BF16)
        ug_ref[g * m : (g + 1) * m, :] = (hg * swish).astype(BF16)
    for c in columns(d, 1024):
        part = lax.dot_general(ge[c, :], gg_ref[...], BY_COLS, preferred_element_type=F32)
        part += lax.dot_general(ue[c, :], ug_ref[...], BY_COLS, preferred_element_type=F32)
        part = part.T
        for g in range(groups):
            owns[g][:, c] = part[g * m : g * m + m // 2]
            sends[g][:, c] = part[g * m + m // 2 : (g + 1) * m].astype(BF16)


def input_grad(acts, hids, ge, ue):
    d, f = ge.shape
    groups, m, n = len(acts), acts[0][0].shape[0], len(acts[0][1])
    outs = [sds((groups * m, f), BF16)] * 2 + [sds((m // 2, d), F32)] * groups + [sds((m // 2, d), BF16)] * groups
    args = [a for own, recvs in (*acts, *hids) for a in (own, *recvs)] + [vm(ge), vm(ue)]
    gg, ug, *rest = call(functools.partial(input_grad_body, groups, n), outs, args, 4 * groups * m * d * f, limit=12)
    return gg, ug, list(zip(rest[:groups], rest[groups:]))


def wgrad_body(nl, nr, factor, aliased, *refs):
    ls, rs, mask = refs[:nl], refs[nl : nl + nr], refs[nl + nr]
    out, right = refs[nl + nr + 1 + aliased :]

    @pl.when(pl.program_id(0) == 0)
    def _():
        stack(right, rs)

    def store(rows, value):
        out[rows, :] = value

    wgrad_block(ls, right, slice(0, out.shape[0]), mask, factor, store)


def wgrad(ls, rs, mask, factor, size, first, count, prev):
    a, b = ls[0].shape[1], rs[0].shape[1]
    m = sum(l.shape[0] for l in ls)
    specs = [pl.BlockSpec((l.shape[0], size), lambda i: (0, first + i)) for l in ls] + [whole(r) for r in rs]
    specs.append(pl.BlockSpec((size // BLOCK, 1, b), lambda i: (first + i, 0, 0)))
    args = (*ls, *rs, mask)
    if prev is not None:
        args, specs = (*args, prev), specs + [HB]
    return call(
        functools.partial(wgrad_body, len(ls), len(rs), factor, int(prev is not None)), [sds((a, b), F32)],
        args, 2 * m * size * count * b, in_specs=specs,
        out_specs=[pl.BlockSpec((size, b), lambda i: (first + i, 0))],
        grid=(count,), scratch=[pltpu.VMEM((m, b), BF16)], limit=16,
        aliases={} if prev is None else {len(args) - 1: 0},
    )[0]


def gather(shard, zs, xs, ticks):
    column = [shard] + [swap(shard, "hid", z) for z in zs[:2]]
    if zs:
        column.append(swap(column[2], "hid", zs[0]))
    groups = [column] + [[swap(p, "hid", x) for p in column] for x in xs]
    if ticks:
        tick(shard)
        tick(column[2])
    halves = [jnp.concatenate(g, axis=0) for g in groups]
    return [(h, swap(h, "hid", 1)) for h in halves]


def scatter(parts, zs, xs, ticks):
    nz = len(zs) + 1
    sums = [own + swap(send, "hid", 1).astype(F32) for own, send in parts]
    rows = sums[0].shape[0] // nz

    def part(i, k):
        return sums[i][k * rows : (k + 1) * rows]

    def sent(x, offset):
        return swap(x.astype(BF16), "hid", offset).astype(F32)

    out = part(0, 0)
    if not zs:
        for j, x in enumerate(xs):
            out = out + sent(part(j + 1, 0), x)
        return out
    one, two = part(0, 1), part(0, 2) + sent(part(0, 3), zs[0])
    for j, x in enumerate(xs):
        two = two + sent(part(j + 1, 2), x)
    two = two.astype(BF16)
    if ticks:
        tick(two)
    for j, x in enumerate(xs):
        one = one + lax.optimization_barrier((sent(part(j + 1, 1), x), two))[0]
        out = out + sent(part(j + 1, 3), x ^ zs[2]) + sent(part(j + 1, 0), x)
    return out + sent(two, zs[1]) + sent(one, zs[0])


def layer(student_in, target_delta, gw, uw, dw, block_mask):
    hid = lax.axis_size("hid")
    nz = 4 if hid % 8 == 0 else 1
    nx = hid // (nz * CORES)
    zs = [k * nx * CORES for k in range(1, nz)]
    xs = [j * CORES for j in range(1, nx)]
    factor = float((student_in.shape[0] * hid) ** -0.5)

    def wide(b):
        return jnp.repeat(b.astype(F32), BLOCK, axis=1)[:, None, :]

    gm, um, dm = wide(block_mask[0]), wide(block_mask[1]), wide(block_mask[2].T)
    ge, ue, de = load(gw, gm), load(uw, um), load(dw, dm)

    inputs = gather(student_in, zs, xs, False)
    acts = []
    for x0, x1 in inputs:
        own, send = gate_up(x0, x1, ge, ue)
        acts.append((own, shifts(send)))
    hiddens, parts = [], []
    for own, recvs in acts:
        h, o, s = down(own, recvs, de)
        hiddens.append(h)
        parts.append((o, s))
    output_sum = scatter(parts, zs, xs, True)
    error = (output_sum - target_delta.astype(F32)).astype(BF16)
    errors = gather(error, zs, xs, True)
    hgs = []
    for e0, e1 in errors:
        own, send = hidden_grad(e0, e1, de)
        hgs.append((own, shifts(send)))
    all_in = [p for x in inputs for p in x]
    all_err = [p for e in errors for p in e]
    d, f = gw.shape
    dsize, gsize = BLOCK, min(512, d)
    down_w = wgrad(hiddens, all_err, dm, factor, dsize, 0, f // dsize, None)
    gg, ug, parts = input_grad(acts, hgs, ge, ue)
    gate_w = wgrad(all_in, [gg], gm, factor, gsize, 0, d // gsize, None)
    up_w = wgrad(all_in, [ug], um, factor, gsize, 0, d // gsize, None)
    grad = scatter(parts, zs, xs, False)
    return (output_sum.astype(BF16), grad.astype(BF16), gate_w, up_w, down_w)


def solution(mesh):
    placed = (
        P("hid", "tok"),
        P("hid", "tok"),
        P("tok", "hid"),
        P("tok", "hid"),
        P("hid", "tok"),
        P(None, "tok", "hid"),
    )
    return jax.shard_map(
        layer,
        mesh=mesh,
        in_specs=placed,
        out_specs=(
            P("hid", "tok"),
            P("hid", "tok"),
            P("tok", "hid"),
            P("tok", "hid"),
            P("hid", "tok"),
        ),
        check_vma=False,
    )
```

```python
import functools
import math

import jax
import jax.numpy as jnp
from jax import lax
from jax.experimental import pallas as pl
from jax.experimental.pallas import tpu as pltpu
from jax.sharding import PartitionSpec as P


BLOCK = 128
CORES = 2
F32, BF16 = jnp.float32, jnp.bfloat16
BY_COLS = (((1,), (1,)), ((), ()))
BY_ROWS = (((0,), (0,)), ((), ()))
MIB = 2**20
VM = pl.BlockSpec(memory_space=pltpu.VMEM)
HB = pl.BlockSpec(memory_space=pl.ANY)


def swap(x, axis, offset):
    n = lax.axis_size(axis)
    return lax.ppermute(x, axis, [(i, i ^ offset) for i in range(n)])


def shifts(x):
    n = lax.axis_size("tok")
    return [lax.ppermute(x, "tok", [(i, (i + d) % n) for i in range(n)]) for d in range(1, n)]


def sds(shape, dtype):
    return jax.ShapeDtypeStruct(shape, dtype)


def call(body, outs, args, flops, in_specs=None, out_specs=None, grid=(), scratch=(), limit=8, effects=False, aliases=None):
    moved = sum(a.size * a.dtype.itemsize for a in args)
    moved += sum(math.prod(o.shape) * jnp.dtype(o.dtype).itemsize for o in outs)
    return pl.pallas_call(
        body,
        grid=grid,
        in_specs=in_specs or [VM] * len(args),
        out_specs=out_specs or [VM] * len(outs),
        out_shape=outs,
        scratch_shapes=list(scratch),
        input_output_aliases=aliases or {},
        cost_estimate=pl.CostEstimate(flops=flops, bytes_accessed=moved, transcendentals=0),
        compiler_params=pltpu.CompilerParams(
            vmem_limit_bytes=limit * MIB,
            has_side_effects=effects,
            dimension_semantics=("arbitrary",) * len(grid) if grid else None,
        ),
    )(*args)


def vm(a):
    return pltpu.with_memory_space_constraint(a, pltpu.VMEM)


def load_body(w, m, out, sems):
    n = sems.shape[0]
    rows = w.shape[0] // n
    copies = [
        pltpu.make_async_copy(w.at[pl.ds(j * rows, rows), :], out.at[pl.ds(j * rows, rows), :], sems.at[j])
        for j in range(n)
    ]
    for c in copies:
        c.start()
    for j in range(n):
        copies[j].wait()

        @pl.loop(0, rows // BLOCK)
        def _(i):
            k = j * (rows // BLOCK) + i
            at = pl.ds(pl.multiple_of(k * BLOCK, BLOCK), BLOCK)
            out[at, :] = out[at, :] * jnp.broadcast_to(m[k].astype(BF16), (BLOCK, w.shape[1]))


def load(w, m):
    parts = 4 if w.shape[0] % (4 * BLOCK) == 0 else 1
    return call(
        load_body, [pltpu.VMEM(w.shape, BF16)], (pltpu.with_memory_space_constraint(w, pltpu.HBM), m), 0,
        in_specs=[HB, VM], scratch=[pltpu.SemaphoreType.DMA((parts,))], limit=4,
    )[0]


def tick_body(x, out):
    out[...] = jnp.zeros_like(out)


def tick(x):
    return call(tick_body, [pltpu.VMEM((8, BLOCK), F32)], (x,), 0, in_specs=[HB], limit=1, effects=True)


def project_body(x0, x1, *refs):
    ws, own, send = refs[:-2], refs[-2], refs[-1]
    x = jnp.concatenate([x0[...], x1[...]], axis=0)
    f = ws[0].shape[1]
    for i, w in enumerate(ws):
        part = jnp.dot(x, w[...], preferred_element_type=F32)
        own[:, i * f : (i + 1) * f] = part
        send[:, i * f : (i + 1) * f] = part.astype(BF16)


def project(x0, x1, ws):
    d, f = ws[0].shape
    m, n = 2 * x0.shape[0], len(ws) * f
    return call(project_body, [sds((m, n), F32), sds((m, n), BF16)], (x0, x1, *map(vm, ws)), 2 * m * d * n)


def total(own, recvs):
    out = own[...]
    for r in recvs:
        out = out + r[...].astype(F32)
    return out


def taken(refs, counts):
    values = []
    for n in counts:
        values.append(total(refs[0], refs[1:n]))
        refs = refs[n:]
    return jnp.concatenate(values, axis=1), refs


def columns(d, n):
    return [slice(c, min(c + n, d)) for c in range(0, d, n)]


def down_body(counts, *refs):
    both, (de, hidden, own, send) = taken(refs, counts)
    f, d = de.shape
    gate, up = both[:, :f], both[:, f:]
    h = (gate * jax.nn.sigmoid(gate) * up).astype(BF16)
    hidden[...] = h
    half = own.shape[0]
    for c in columns(d, 1024):
        part = jnp.dot(h, de[:, c], preferred_element_type=F32)
        own[:, c] = part[:half]
        send[:, c] = part[half:].astype(BF16)


def down(parts, de):
    f, d = de.shape
    m = parts[0][0].shape[0]
    outs = [sds((m, f), BF16), sds((m // 2, d), F32), sds((m // 2, d), BF16)]
    args = [a for p in parts for a in p] + [vm(de)]
    return call(functools.partial(down_body, [len(p) for p in parts]), outs, args, 2 * m * d * f)


def hidden_grad_body(e0, e1, de, own, send):
    e = jnp.concatenate([e0[...], e1[...]], axis=0)
    for c in columns(de.shape[0], 512):
        part = lax.dot_general(de[c, :], e, BY_COLS, preferred_element_type=F32).T
        own[:, c] = part
        send[:, c] = part.astype(BF16)


def hidden_grad(e0, e1, de):
    f, d = de.shape
    m = 2 * e0.shape[0]
    outs = [sds((m, f), F32), sds((m, f), BF16)]
    return call(hidden_grad_body, outs, (e0, e1, vm(de)), 2 * m * d * f)


def stack(dst, pieces):
    row = 0
    for p in pieces:
        dst[row : row + p.shape[0], :] = p[...]
        row += p.shape[0]


def input_grad_body(acts, hids, *refs):
    values = []
    for counts in (*acts, *hids):
        value, refs = taken(refs, counts)
        values.append(value)
    groups = len(acts)
    ge, ue, gg_ref, ug_ref = refs[:4]
    owns, sends = refs[4 : 4 + groups], refs[4 + groups :]
    d, f = ge.shape
    m = gg_ref.shape[0] // groups
    for g, (both, hg) in enumerate(zip(values[:groups], values[groups:])):
        gate, up = both[:, :f], both[:, f:]
        sigma = jax.nn.sigmoid(gate)
        swish = gate * sigma
        gg_ref[g * m : (g + 1) * m, :] = (hg * up * (sigma + swish * (1.0 - sigma))).astype(BF16)
        ug_ref[g * m : (g + 1) * m, :] = (hg * swish).astype(BF16)
    for c in columns(d, 1024):
        part = lax.dot_general(ge[c, :], gg_ref[...], BY_COLS, preferred_element_type=F32)
        part += lax.dot_general(ue[c, :], ug_ref[...], BY_COLS, preferred_element_type=F32)
        part = part.T
        for g in range(groups):
            owns[g][:, c] = part[g * m : g * m + m // 2]
            sends[g][:, c] = part[g * m + m // 2 : (g + 1) * m].astype(BF16)


def input_grad(acts, hids, ge, ue):
    d, f = ge.shape
    groups, m = len(acts), acts[0][0][0].shape[0]
    outs = [sds((groups * m, f), BF16)] * 2 + [sds((m // 2, d), F32)] * groups + [sds((m // 2, d), BF16)] * groups
    args = [a for parts in (*acts, *hids) for p in parts for a in p] + [vm(ge), vm(ue)]
    counts = [[[len(p) for p in parts] for parts in group] for group in (acts, hids)]
    gg, ug, *rest = call(
        functools.partial(input_grad_body, *counts), outs, args, 4 * groups * m * d * f,
        limit=max(8, groups * m // 64),
    )
    return gg, ug, list(zip(rest[:groups], rest[groups:]))


def wgrad_body(nl, jobs, factor, aliased, *refs):
    ls, refs = refs[:nl], refs[nl:]
    work = []
    for nr in jobs:
        work.append((refs[:nr], refs[nr]))
        refs = refs[nr + 1 :]
    refs = refs[aliased:]
    outs, rights = refs[: len(jobs)], refs[len(jobs) :]

    @pl.when(pl.program_id(0) == 0)
    def _():
        for (rs, _), right in zip(work, rights):
            stack(right, rs)

    left = jnp.concatenate([l[...] for l in ls], axis=0)
    for (_, mask), out, right in zip(work, outs, rights):
        w = lax.dot_general(left, right[...], BY_ROWS, preferred_element_type=F32)
        for k in range(out.shape[0] // BLOCK):
            rows = slice(k * BLOCK, (k + 1) * BLOCK)
            out[rows, :] = w[rows, :] * (mask[k] * factor)


def wgrad(ls, jobs, factor, size, first, count, prev):
    a, b = ls[0].shape[1], jobs[0][0][0].shape[1]
    m, n = sum(l.shape[0] for l in ls), len(jobs)
    specs = [pl.BlockSpec((l.shape[0], size), lambda i: (0, first + i)) for l in ls]
    args = list(ls)
    for rs, mask in jobs:
        args += [*rs, mask]
        specs += [VM for r in rs] + [pl.BlockSpec((size // BLOCK, 1, b), lambda i: (first + i, 0, 0))]
    aliases = {}
    for i, p in enumerate(prev or ()):
        aliases[len(args)] = i
        args.append(p)
        specs.append(HB)
    return call(
        functools.partial(wgrad_body, len(ls), [len(rs) for rs, _ in jobs], factor, len(aliases)),
        [sds((a, b), F32)] * n, tuple(args), 2 * m * size * count * b * n, in_specs=specs,
        out_specs=[pl.BlockSpec((size, b), lambda i: (first + i, 0))] * n,
        grid=(count,), scratch=[pltpu.VMEM((m, b), BF16)] * n, limit=12, aliases=aliases,
    )


def gather(shard, zs, xs, ticks, split):
    column = [shard] + [swap(shard, "hid", z) for z in zs[:2]]
    if zs:
        column.append(swap(column[2], "hid", zs[0]))
    groups = [column] + [[swap(p, "hid", x) for p in column] for x in xs]
    if ticks:
        tick(column[1])
        tick(column[2])
    out = []
    for i, g in enumerate(groups):
        n = len(g) // (split if i == 0 and len(g) % split == 0 else 1)
        rows = [jnp.concatenate(g[j : j + n], axis=0) for j in range(0, len(g), n)]
        out.append([(r, swap(r, "hid", 1)) for r in rows])
    return out


def rows_of(groups):
    return [part[c] for parts in groups for c in (0, 1) for part in parts]


def scatter(parts, zs, xs, ticks):
    nz = len(zs) + 1
    sums = [own + swap(send, "hid", 1).astype(F32) for own, send in parts]
    rows = sums[0].shape[0] // nz

    def part(i, k):
        return sums[i][k * rows : (k + 1) * rows]

    def sent(x, offset):
        return swap(x.astype(BF16), "hid", offset).astype(F32)

    out = part(0, 0)
    if not zs:
        for j, x in enumerate(xs):
            out = out + sent(part(j + 1, 0), x)
        return out
    one, two = part(0, 1), part(0, 2) + sent(part(0, 3), zs[0])
    for j, x in enumerate(xs):
        two = two + sent(part(j + 1, 2), x)
    two = two.astype(BF16)
    if ticks:
        tick(two)
    for j, x in enumerate(xs):
        one = one + lax.optimization_barrier((sent(part(j + 1, 1), x), two))[0]
        out = out + sent(part(j + 1, 3), x ^ zs[2]) + sent(part(j + 1, 0), x)
    return out + sent(two, zs[1]) + sent(one, zs[0])


def layer(student_in, target_delta, gw, uw, dw, block_mask):
    hid = lax.axis_size("hid")
    nz = 4 if hid % 8 == 0 else 1
    nx = hid // (nz * CORES)
    zs = [k * nx * CORES for k in range(1, nz)]
    xs = [j * CORES for j in range(1, nx)]
    factor = float((student_in.shape[0] * hid) ** -0.5)

    def wide(b):
        return jnp.repeat(b.astype(F32), BLOCK, axis=1)[:, None, :]

    gm, um, dm = wide(block_mask[0]), wide(block_mask[1]), wide(block_mask[2].T)
    ge, ue, de = load(gw, gm), load(uw, um), load(dw, dm)

    inputs = gather(student_in, zs, xs, False, 1)
    acts = []
    for ((x0, x1),) in inputs:
        group = []
        for ws in ([ge, ue],):
            own, send = project(x0, x1, ws)
            group.append((own, *shifts(send)))
        acts.append(group)
    hiddens, parts = [], []
    for group in acts:
        h, o, s = down(group, de)
        hiddens.append(h)
        parts.append((o, s))
    output_sum = scatter(parts, zs, xs, True)
    error = (output_sum - target_delta.astype(F32)).astype(BF16)
    errors = gather(error, zs, xs, True, 1)
    hgs = []
    for ((e0, e1),) in errors:
        own, send = hidden_grad(e0, e1, de)
        hgs.append([(own, *shifts(send))])
    all_in, all_err = rows_of(inputs), rows_of(errors)
    d, f = gw.shape
    (down_w,) = wgrad(hiddens, [(all_err, dm)], factor, BLOCK, 0, f // BLOCK, None)
    gg, ug, parts = input_grad(acts, hgs, ge, ue)
    jobs, size = [([gg], gm), ([ug], um)], min(256, d // 2)
    steps = d // size // 2
    early = wgrad(all_in, jobs, factor, size, 0, steps, None)
    gate_w, up_w = wgrad(all_in, jobs, factor, size, steps, steps, early)
    grad = scatter(parts, zs, xs, False)
    return (output_sum.astype(BF16), grad.astype(BF16), gate_w, up_w, down_w)


def solution(mesh):
    placed = (
        P("hid", "tok"),
        P("hid", "tok"),
        P("tok", "hid"),
        P("tok", "hid"),
        P("hid", "tok"),
        P(None, "tok", "hid"),
    )
    return jax.shard_map(
        layer,
        mesh=mesh,
        in_specs=placed,
        out_specs=(
            P("hid", "tok"),
            P("hid", "tok"),
            P("tok", "hid"),
            P("tok", "hid"),
            P("hid", "tok"),
        ),
        check_vma=False,
    )
```
